128 devices in a mesh: row: 16 (over y, x), col: 8 (over z, core).
Axes of the slice: x: 4, y: 4, z: 4, core: 2. Of those that a mesh axis runs over, the one named last changes fastest.
Arguments:
- amplitudes: float32 [16384, 3072], P('row', 'col'), may hold values from -6 to 6
- row_gap: float32 [16384], P('row'), may hold values from -4 to -0.5
- row_irrep: int32 [16384], P('row'), may hold values from 0 to 7
- owners: int32 [16384, 1], P('row'), may hold values from 0 to 15; in each aligned block of 1024 rows (0 to 1023, 1024 to 2047, ...) at most 128 rows name the same one
- stored: float32 [3072, 8192], P('row', 'col'), may hold values from -0.109375 to 0.109375
- col_gap: float32 [8192], P('col'), may hold values from -4 to -0.5
- col_irrep: int32 [8192], P('col'), may hold values from 0 to 7
- mirror_flags: int32 [8], replicated, may hold values from 0 to 1
Outputs:
- update: float32 [32768, 8192], P('row', 'col')
The draws below stay inside these ranges and needn't reach their ends.
Inputs may be any that keep to these rules, and one draw needn't show every extreme that they name: `owners`: in each aligned block of 1024 pairs (the pairs of one row index) no owner is named by more than 128 pairs, a bound that some block reaches.
All inputs are finite; a program needn't handle non-finite values.
Results may differ from the reference program's by a relative error of at most 0.000094.
Values sent between devices are 32-bit elements; how exact they have to be, the bound alone decides.
A program may use at most 128 MiB of HBM per device.

```python
import math
import jax
import jax.numpy as jnp
import numpy as np
from jax import lax

KDIM = 3072
ROWS = 1024
COLS = 1024
CAP = 128
PAIRS_IA = 16384
PAIRS_JB = 8192
N_ROW = 16
N_COL = 8


def with_ends(result, rng, least, top_value):
    extent = result.shape
    spot = [jax.random.randint(jax.random.fold_in(rng, axis), (), 0, extent[axis]) for axis in range(len(extent))]
    result = result.at[tuple(spot)].set(least)
    longest = extent.index(max(extent))
    spot[longest] = (spot[longest] + 1) % extent[longest]
    return result.at[tuple(spot)].set(top_value)


def block_levels(key, dims, cuts, least, high):
    def one(axis_at, blocks):
        heights = jax.random.uniform(jax.random.fold_in(jax.random.fold_in(key, 6), axis_at), (blocks,), jnp.float32, least / len(cuts), high / len(cuts))
        return jnp.repeat(jnp.exp(heights), dims[axis_at] // blocks).reshape((-1,) + (1,) * (len(dims) - axis_at - 1))

    loudness = one(*cuts[0])
    for cut in cuts[1:]:
        loudness = loudness * one(*cut)
    return loudness


def shared_out(rng, own, number, rows, number_of, top, reach, slope):
    sequence = jax.random.permutation(rng, number_of)
    crowded, common = load_shares(number_of, rows * top, reach, slope, True), load_shares(number_of, rows * top, reach, slope, False)
    places = jnp.arange(number_of)

    def named(sizes, offset_by):
        used = int((sizes > 0).sum())
        fixed = max(1, used // 4)
        passed = fixed + (places - fixed + offset_by * (used - fixed)) % max(1, number_of - fixed)
        return jnp.zeros((number_of,), jnp.int32).at[sequence[jnp.where(places < fixed, places, passed)]].set(jnp.asarray(sizes, jnp.int32))

    sizes = jnp.where(number % 4 == 0, named(crowded, number // 4), named(common, number - number // 4 - 1))
    mixed = jax.random.permutation(jax.random.fold_in(own, 3), number_of)
    giver, sink = mixed[0:number_of // 2 * 2:2], mixed[1:number_of // 2 * 2:2]
    room = jnp.minimum(sizes[giver] - 1, reach - sizes[sink]) // 2
    room = jnp.where((giver == sequence[0]) | (sink == sequence[0]) | (sizes[sink] == 0), 0, jnp.maximum(room, 0))
    passed = jax.random.randint(jax.random.fold_in(own, 4), (number_of // 2,), 0, 1 << 20) % (room + 1)
    sizes = sizes.at[giver].add(-passed).at[sink].add(passed)
    items = jnp.searchsorted(jnp.cumsum(sizes), jnp.arange(rows * top), side="right").astype(jnp.int32)
    grid = items.reshape(top, rows).T
    grid = grid[jax.random.permutation(jax.random.fold_in(own, 1), rows)]
    offset_by = jax.random.randint(jax.random.fold_in(own, 2), (rows, 1), 0, top)
    return jnp.take_along_axis(grid, (jnp.arange(top)[None, :] + offset_by) % top, axis=1)


def load_shares(amount, total, most, lean, full):
    weights = [(1 << 20) // math.isqrt(standing ** lean) + 1 for standing in range(1, amount + 1)]
    largest = most if full else min(most, max(-(-total // amount), total * weights[0] // sum(weights)))
    least = 1 if total - largest >= amount - 1 else 0
    holding, rest = [largest] + [least] * (amount - 1), total - largest - least * (amount - 1)
    while rest > 0:
        candidates = [i for i in range(1, amount) if holding[i] < largest] or [i for i in range(1, amount) if holding[i] < most]
        mass, budget = sum([weights[i] for i in candidates]), rest
        for i in candidates:
            addition = min(most - holding[i], max(1, budget * weights[i] // mass), rest)
            holding[i] = holding[i] + addition
            rest = rest - addition
    return np.array(holding)


def noise(key, dims, width, most, split=(), kind=jnp.bfloat16):
    factor_of = block_levels(key, dims, split, -0.22, 0.18) if split else 1.0
    result = jax.random.normal(key, dims, jnp.float32) * width * factor_of
    return jnp.minimum(jnp.maximum(result, -most), most).astype(kind)


def setup_inputs(seed: int = 0) -> dict:
    seeds = jax.random.split(jax.random.key(seed), 9)
    amplitudes = noise(seeds[0], (PAIRS_IA, KDIM), 1.0, 6.0, ((0, 16), (1, 8)), jnp.float32)
    row_gap = jnp.clip(-4.0 + 3.5 * jax.random.uniform(seeds[1], (PAIRS_IA,), jnp.float32) ** block_levels(seeds[1], (PAIRS_IA,), ((0, 16),), -0.2, 0.2), -4.0, -0.5)
    row_irrep = with_ends(jax.random.randint(seeds[2], (PAIRS_IA,), 0, 8), jax.random.fold_in(seeds[2], 1), 0, 7).astype(jnp.int32)
    owners_keys = jax.random.split(jax.random.fold_in(seeds[3], 1), PAIRS_IA // ROWS)
    owners_turns = jax.random.permutation(jax.random.fold_in(seeds[3], 3), PAIRS_IA // ROWS)
    owners = jax.vmap(lambda own, number: shared_out(jax.random.fold_in(seeds[3], 2), own, number, ROWS, N_ROW, 1, CAP, 2))(owners_keys, owners_turns).reshape((PAIRS_IA, 1))
    stored = noise(seeds[4], (KDIM, PAIRS_JB), KDIM ** -0.5, 0.109375, ((0, 16), (1, 8)), jnp.float32)
    col_gap = jnp.clip(-4.0 + 3.5 * jax.random.uniform(seeds[5], (PAIRS_JB,), jnp.float32) ** block_levels(seeds[5], (PAIRS_JB,), ((0, 8),), -0.2, 0.2), -4.0, -0.5)
    col_irrep = with_ends(jax.random.randint(seeds[6], (PAIRS_JB,), 0, 8), jax.random.fold_in(seeds[6], 1), 0, 7).astype(jnp.int32)
    mirror_flags = with_ends(jax.random.randint(seeds[7], (N_COL,), 0, 2), jax.random.fold_in(seeds[7], 1), 0, 1).astype(jnp.int32)
    return dict(amplitudes=amplitudes, row_gap=row_gap, row_irrep=row_irrep, owners=owners, stored=stored, col_gap=col_gap, col_irrep=col_irrep, mirror_flags=mirror_flags)


def reference(amplitudes, row_gap, row_irrep, owners, stored, col_gap, col_irrep, mirror_flags):
    half = (N_COL // 2) * COLS
    parity = jnp.repeat(1 - 2 * mirror_flags, COLS).astype(jnp.float32)
    weights = stored + parity[None, :] * jnp.roll(stored, half, axis=1)
    cycle = jnp.dot(amplitudes, weights, precision=lax.Precision.HIGHEST, preferred_element_type=jnp.float32)
    same = row_irrep[:, None] == col_irrep[None, :]
    values = jnp.where(same, cycle / (row_gap[:, None] + col_gap[None, :]), jnp.zeros_like(cycle))
    target = owners[:, 0].astype(jnp.int32)
    onehot = (target.reshape(N_ROW, ROWS)[:, :, None] == jnp.arange(N_ROW, dtype=jnp.int32)[None, None, :]).astype(jnp.int32)
    running = jnp.cumsum(onehot, axis=1) - onehot
    slot_index = jnp.sum(running * onehot, axis=2).reshape(-1).astype(jnp.int32)
    source = (jnp.arange(N_ROW * ROWS, dtype=jnp.int32) // ROWS).astype(jnp.int32)
    index = (target * (N_ROW * CAP) + source * CAP + slot_index).astype(jnp.int32)
    update = jnp.zeros((N_ROW * N_ROW * CAP, N_COL * COLS), jnp.float32)
    return update.at[index].set(values)
```

```python
import jax
import jax.numpy as jnp
from jax import lax
from jax.sharding import PartitionSpec as P


def from_partner(value, axis, distance):
    mask = 2**distance
    pairs = [(source, source ^ mask) for source in range(lax.axis_size(axis))]
    return lax.ppermute(value, axis, pairs)


def send_positions(target, row_count, capacity):
    onehot = (target[:, None] == jnp.arange(row_count, dtype=jnp.int32)[None, :]).astype(jnp.float32)
    count = target.shape[0]
    place = jnp.arange(count, dtype=jnp.int32)
    earlier = (place[None, :] < place[:, None]).astype(jnp.float32)
    running = jnp.dot(earlier, onehot, preferred_element_type=jnp.float32)
    slot_index = jnp.sum(running * onehot, axis=1).astype(jnp.int32)
    return target * capacity + slot_index


def per_device(amplitudes, row_gap, row_irrep, owners, stored, col_gap, col_irrep, mirror_flags):
    row_count = lax.axis_size("row")
    local_rows = amplitudes.shape[0]
    capacity = 2 * local_rows // row_count
    slot_total = row_count * capacity
    positions = send_positions(owners[:, 0], row_count, capacity)
    gathered = lax.all_gather(amplitudes, "col", axis=1, tiled=True)
    parity = (1 - 2 * mirror_flags[lax.axis_index("col")]).astype(jnp.float32)
    mirror_bit = lax.axis_size("col").bit_length() - 2
    operand = stored + parity * from_partner(stored, "col", mirror_bit)
    product = jnp.dot(
        gathered,
        lax.all_gather(operand, "row", axis=0, tiled=True),
        precision=lax.Precision.HIGH,
        preferred_element_type=jnp.float32,
    )
    same = row_irrep[:, None] == col_irrep[None, :]
    values = jnp.where(same, product / (row_gap[:, None] + col_gap[None, :]), jnp.zeros_like(product))
    buffer = jnp.zeros((slot_total, values.shape[1]), jnp.float32).at[positions].set(values)
    return lax.all_to_all(buffer, "row", split_axis=0, concat_axis=0, tiled=True)


def solution(mesh):
    placed = (
        P("row", "col"),
        P("row"),
        P("row"),
        P("row", None),
        P("row", "col"),
        P("col"),
        P("col"),
        P(),
    )
    return jax.shard_map(
        per_device, mesh=mesh, in_specs=placed, out_specs=P("row", "col"), check_vma=False
    )
```

```python
import jax
import jax.numpy as jnp
from jax import lax
from jax.experimental import pallas as pl
from jax.experimental.pallas import tpu as pltpu
from jax.sharding import PartitionSpec as P

SIDE = 4
STEPS = (0, 1, 3, 2)
DEPTH = 3072
LANES = 1024
PART = 384
CHUNK = 192
ROWS = 1024
CAP = 128
HALF = LANES // 2
GROUP = SIDE * CAP
CORES = 2


def plan():
    copies = {}
    for h in range(2):
        copies["mirror", h] = ((0, 0, 2, 0), [], 384)
    for g, dy in enumerate(STEPS):
        for dx in range(SIDE):
            if dy or dx:
                copies["meta", g, dx] = ((-dy, -dx, 0, 0), [], 4)
                copies["route", g, dx] = ((-dy, -dx, 0, 0), [], 192)
    for h in range(2):
        own = [("mirror", h)]

        def along(axis, step, h=h):
            first = (axis == 0) == (h == 0)
            return (0, step, 0, 0) if first else (step, 0, 0, 0)

        for s in (1, -1):
            copies["line", h, s] = (along(0, s), own, 384)
            copies["linepass", h, s] = (along(0, s), [("line", h, s)], 192)
        for j in (0, -1, 1, 2):
            if j == 0:
                after = own
            elif j == 2:
                after = [("linepass", h, 1), ("linepass", h, -1)]
            else:
                after = [("line", h, -j)]
            for s in (1, -1):
                copies["plane", h, j, s] = (along(1, s), after, 384)
                copies["planepass", h, j, s] = (along(1, s), [("plane", h, j, s)], 192)
    for g, dy in enumerate(STEPS):
        here = [("route", g, dx) for dx in range(SIDE) if dy or dx]
        copies["own", g] = ((0, 0, 0, 1), here, 768)
        for s in (1, -1):
            copies["ring", g, s] = ((0, 0, s, 0), here, 768)
            copies["ringpass", g, s] = ((0, 0, s, 0), [("ring", g, s)], 384)
            copies["share", g, s] = ((0, 0, 0, 1), [("ring", g, s)], 768)
            copies["sharepass", g, s] = ((0, 0, 0, 1), [("ringpass", g, s)], 384)
    return copies


def arrivals(copies):
    free, arrived, issued = {}, {}, {}
    ready = {}
    slot = 0
    for name, (_, after, _) in copies.items():
        if not after:
            if name[0] == "mirror":
                ready[name] = 3.0
            else:
                slot += 1
                ready[name] = 4.0 + 0.25 * slot
    while len(issued) < len(copies):
        name = min((n for n in ready if n not in issued), key=lambda n: (ready[n], str(n)))
        issued[name] = at = ready[name]
        offset, _, size = copies[name]
        end = at
        for axis, step in enumerate(offset):
            step = (step + 1) % SIDE - 1 if axis < 3 else step
            ways = ((1, 0.5), (-1, 0.5)) if abs(step) == 2 else ((step, 1.0),)
            for way, share in ways:
                if step:
                    link = (axis, way > 0)
                    hops = abs(step)
                    rate = 400.0 if axis == 3 else 43.0
                    start = max(at, free.get(link, 0.0))
                    free[link] = start + 1.05 * size * share * hops / rate
                    end = max(end, free[link])
        arrived[name] = end + 2.0
        for other, (_, after, _) in copies.items():
            if other not in ready and after and all(a in arrived for a in after):
                ready[other] = max(arrived[a] for a in after) + 0.5
    return sorted(copies, key=lambda n: (arrived[n], str(n)))


def kernel(
    amp, own, gap, irrep, stored, flags, cycle, meta,
    slots, weights, high, low, outgoing, mirrored, places, notes, heard, sent, came, done,
):
    row, col = lax.axis_index("row"), lax.axis_index("col")
    y, x, z, k = row // SIDE, row % SIDE, col // CORES, col % CORES

    def device(offset):
        dy, dx, dz, dk = offset
        there = ((y + dy + SIDE) % SIDE) * SIDE + (x + dx + SIDE) % SIDE
        return {"row": there, "col": ((z + dz + SIDE) % SIDE) * CORES + (k + dk) % CORES}

    copies = plan()
    index = {name: i for i, name in enumerate(copies)}
    barrier = pltpu.get_barrier_semaphore()
    partners = [(dy, dx, 0, 0) for dy in range(SIDE) for dx in range(SIDE) if dy or dx]
    partners += [(0, 0, 1, 0), (0, 0, 2, 0), (0, 0, 3, 0), (0, 0, 0, 1)]
    for offset in partners:
        pl.semaphore_signal(barrier, inc=1, device_id=device(offset), device_id_type=pl.DeviceIdType.MESH)

    def chunk(h, p, q, part):
        dx, dy = (p, q) if h == 0 else (q, p)
        at = (((y + dy + SIDE) % SIDE) * SIDE + (x + dx + SIDE) % SIDE) * CHUNK
        size = CHUNK if part == 0 else CHUNK // 2
        at = at + (CHUNK // 2 if part < 0 else 0)
        return pl.ds(pl.multiple_of(at, CHUNK // 2), size), pl.ds(h * HALF, HALF)

    def group(dy):
        return ((y + dy) % SIDE) * SIDE

    def held(dz, g, part):
        at = group(STEPS[g]) + (SIDE // 2 if part < 0 else 0)
        size = SIDE if part == 0 else SIDE // 2
        return slots.at[((z + dz + SIDE) % SIDE) * CORES + k, pl.ds(at, size)]

    made = {}

    def copy(name):
        if name in made:
            return made[name]
        kind, rest = name[0], name[1:]
        if kind == "mirror":
            cols = pl.ds(rest[0] * HALF, HALF)
            src, dst = stored.at[:, cols], mirrored.at[:, cols]
        elif kind == "meta":
            i = rest[0] * SIDE + rest[1]
            src, dst = notes.at[i], heard.at[row]
        elif kind == "route":
            i = rest[0] * SIDE + rest[1]
            src, dst = outgoing.at[i], slots.at[col, row]
        elif kind in ("line", "linepass", "plane", "planepass"):
            h, s = rest[0], rest[-1]
            if kind == "line":
                where = chunk(h, 0, 0, 0)
            elif kind == "linepass":
                where = chunk(h, -s, 0, s)
            elif kind == "plane":
                where = chunk(h, rest[1], 0, 0)
            else:
                where = chunk(h, rest[1], -s, s)
            src = dst = weights.at[where]
        else:
            g = rest[0]
            if kind in ("own",):
                src = held(0, g, 0)
            elif kind == "ring":
                src = held(0, g, 0)
            elif kind == "ringpass":
                src = held(-rest[1], g, rest[1])
            elif kind == "share":
                src = held(-rest[1], g, 0)
            else:
                src = held(2, g, rest[1])
            dst = src
        i = index[name]
        made[name] = pltpu.make_async_remote_copy(
            src_ref=src, dst_ref=dst, send_sem=sent.at[i], recv_sem=came.at[i],
            device_id=device(copies[name][0]), device_id_type=pl.DeviceIdType.MESH,
        )
        return made[name]

    def halves(value):
        top = value.astype(jnp.bfloat16)
        return top, (value - top.astype(jnp.float32)).astype(jnp.bfloat16)

    earlier = (
        lax.broadcasted_iota(jnp.int32, (CAP, CAP), 0) < lax.broadcasted_iota(jnp.int32, (CAP, CAP), 1)
    ).astype(jnp.float32).astype(jnp.bfloat16)
    count = jnp.zeros((16, 1), jnp.float32)
    for b in range(ROWS // CAP):
        names = own[:, b * CAP : (b + 1) * CAP]
        hit = lax.broadcasted_iota(jnp.int32, (16, CAP), 0) == names
        one = jnp.where(hit, 1.0, 0.0)
        running = jnp.dot(one.astype(jnp.bfloat16), earlier, preferred_element_type=jnp.float32) + count
        places[:, b * CAP : (b + 1) * CAP] = jnp.where(hit, running, -1.0)
        count = count + jnp.sum(one, axis=1, keepdims=True)

    high[0:ROWS, 0:PART], low[0:ROWS, 0:PART] = halves(amp[...])
    gap_top, gap_rest = halves(gap[...])
    gap_rest = gap[...] - gap_top.astype(jnp.float32)
    gap_mid, gap_end = halves(gap_rest)
    pieces = [
        gap_top.astype(jnp.float32),
        gap_mid.astype(jnp.float32),
        gap_end.astype(jnp.float32),
        (irrep[...] + 1).astype(jnp.float32),
    ]
    tags = jnp.concatenate(pieces + [jnp.zeros((12, ROWS), jnp.float32)], axis=0).astype(jnp.bfloat16)

    pl.semaphore_wait(barrier, len(partners))
    started = []

    def start(name):
        copy(name).start()
        started.append(name)

    for h in range(2):
        start(("mirror", h))

    def slotted(owner):
        place = places[pl.ds(owner, 1), :]
        pick = lax.broadcasted_iota(jnp.int32, (CAP, ROWS), 0).astype(jnp.float32) == place
        pick = jnp.where(pick, 1.0, 0.0).astype(jnp.bfloat16)
        block = jnp.dot(pick, high[0:ROWS, 0:PART], preferred_element_type=jnp.float32)
        block += jnp.dot(pick, low[0:ROWS, 0:PART], preferred_element_type=jnp.float32)
        note = lax.dot_general(tags, pick, (((1,), (1,)), ((), ())), preferred_element_type=jnp.float32)
        return block, note[0:8]

    for g, dy in enumerate(STEPS):
        for dx in range(SIDE):
            there = ((y - dy + SIDE) % SIDE) * SIDE + (x - dx + SIDE) % SIDE
            block, note = slotted(there)
            i = g * SIDE + dx
            if i == 0:
                slots[col, row] = block
                heard[row] = note
            else:
                outgoing[i] = block
                notes[i] = note
                start(("route", g, dx))
                start(("meta", g, dx))

    parity = (1 - 2 * flags[col]).astype(jnp.float32)

    def split(where, n):
        rows, cols = where
        first = rows.start

        def body(i, carry):
            at = pl.ds(pl.multiple_of(first + i * 32, 32), 32)
            high[at, cols], low[at, cols] = halves(weights[at, cols])
            return carry

        lax.fori_loop(0, n // 32, body, 0)

    def multiply(g, offsets):
        base = g * GROUP

        def body(i, carry):
            dz = jnp.int32(0)
            for n, o in enumerate(offsets):
                dz = jnp.where(i // CORES == n, o, dz)
            c = ((z + dz + SIDE) % SIDE) * CORES + i % CORES
            a = slots[c, pl.ds(group(STEPS[g]), SIDE)].reshape(GROUP, PART)
            top, rest = halves(a)
            at = pl.ds(pl.multiple_of(c * PART, PART), PART)
            for n in range(0, LANES, 256):
                w = high[at, n : n + 256]
                add = jnp.dot(top, w, preferred_element_type=jnp.float32)
                add += jnp.dot(rest, w, preferred_element_type=jnp.float32)
                add += jnp.dot(top, low[at, n : n + 256], preferred_element_type=jnp.float32)
                weights[base : base + GROUP, n : n + 256] += add
            return carry

        lax.fori_loop(0, len(offsets) * CORES, body, 0)

    def write(g):
        return pltpu.make_async_copy(
            weights.at[pl.ds(g * GROUP, GROUP)],
            cycle.at[pl.ds(pl.multiple_of(group(STEPS[g]) * CAP, GROUP), GROUP)],
            done.at[g],
        )

    seen = set()
    weight_kinds = ("line", "linepass", "plane", "planepass")
    left_weights = sum(n[0] in weight_kinds for n in copies)
    computed = {}
    near, far = (0, -1, 1), (2,)

    def has(g, offsets):
        need = [("route", g, dx) for dx in range(SIDE) if STEPS[g] or dx]
        need += [("own", g)]
        for s in (1, -1):
            if -s in offsets:
                need += [("ring", g, s), ("share", g, s)]
            if 2 in offsets:
                need += [("ringpass", g, s), ("sharepass", g, s)]
        return all(n in seen for n in need)

    def run_ready():
        if left_weights:
            return
        for g in range(SIDE):
            stage = computed.get(g, 0)
            if stage == 0 and has(g, near + far):
                weights[g * GROUP : (g + 1) * GROUP] = jnp.zeros((GROUP, LANES), jnp.float32)
                multiply(g, near + far)
                write(g).start()
                computed[g] = 2
            elif stage == 0 and g == SIDE - 1 and has(g, near):
                weights[g * GROUP : (g + 1) * GROUP] = jnp.zeros((GROUP, LANES), jnp.float32)
                multiply(g, near)
                computed[g] = 1
            elif stage == 1 and has(g, far):
                multiply(g, far)
                write(g).start()
                computed[g] = 2

    for name in arrivals(copies):
        copy(name).wait_recv()
        seen.add(name)
        kind = name[0]
        if kind == "mirror":
            cols = pl.ds(name[1] * HALF, HALF)
            mine = chunk(name[1], 0, 0, 0)
            weights[mine] = stored[:, cols] + parity * mirrored[:, cols]
        for other, (_, after, _) in copies.items():
            if other not in started and after and name in after and all(a in seen for a in after):
                start(other)
        if kind == "mirror":
            split(mine, CHUNK)
        if kind in weight_kinds:
            left_weights -= 1
            h, s = name[1], name[-1]
            if kind == "line":
                split(chunk(h, -s, 0, 0), CHUNK)
            elif kind == "linepass":
                split(chunk(h, -2 * s, 0, s), CHUNK // 2)
            elif kind == "plane":
                split(chunk(h, name[2], -s, 0), CHUNK)
            else:
                split(chunk(h, name[2], -2 * s, s), CHUNK // 2)
            if left_weights == 0:
                for n in copies:
                    if n[0] in weight_kinds:
                        copy(n).wait_send()
        run_ready()

    for i in range(16):
        meta[i] = heard[i]
    for n in copies:
        if n[0] not in weight_kinds:
            copy(n).wait_send()
    for g in range(SIDE):
        write(g).wait()


def exchange(amp, own, gap, irrep, stored, flags):
    n = len(plan())
    vmem = pl.BlockSpec(memory_space=pltpu.VMEM)
    return pl.pallas_call(
        kernel,
        out_shape=(
            jax.ShapeDtypeStruct((16 * CAP, LANES), jnp.float32),
            jax.ShapeDtypeStruct((16, 8, CAP), jnp.float32),
        ),
        in_specs=[vmem] * 5 + [pl.BlockSpec(memory_space=pltpu.SMEM)],
        out_specs=(pl.BlockSpec(memory_space=pl.ANY), vmem),
        scratch_shapes=[
            pltpu.VMEM((SIDE * CORES, 16, CAP, PART), jnp.float32),
            pltpu.VMEM((DEPTH, LANES), jnp.float32),
            pltpu.VMEM((DEPTH, LANES), jnp.bfloat16),
            pltpu.VMEM((DEPTH, LANES), jnp.bfloat16),
            pltpu.VMEM((16, CAP, PART), jnp.float32),
            pltpu.VMEM((CHUNK, LANES), jnp.float32),
            pltpu.VMEM((16, ROWS), jnp.float32),
            pltpu.VMEM((16, 8, CAP), jnp.float32),
            pltpu.VMEM((16, 8, CAP), jnp.float32),
            pltpu.SemaphoreType.DMA((n,)),
            pltpu.SemaphoreType.DMA((n,)),
            pltpu.SemaphoreType.DMA((SIDE,)),
        ],
        compiler_params=pltpu.CompilerParams(
            collective_id=0, has_side_effects=True, vmem_limit_bytes=60 * 2**20
        ),
        name="exchange",
    )(amp, own, gap, irrep, stored, flags)


def per_device(amplitudes, row_gap, row_irrep, owners, stored, col_gap, col_irrep, mirror_flags):
    line = (1, ROWS)
    cycle, meta = exchange(
        amplitudes, owners.reshape(line), row_gap.reshape(line), row_irrep.reshape(line), stored, mirror_flags
    )
    gap = (meta[:, 0] + meta[:, 1] + meta[:, 2]).reshape(-1, 1)
    irrep = (meta[:, 3] - 1.0).reshape(-1, 1)
    same = irrep == col_irrep.astype(jnp.float32)[None, :]
    return jnp.where(same, cycle / (gap + col_gap[None, :]), 0.0)


def solution(mesh):
    placed = (
        P("row", "col"),
        P("row"),
        P("row"),
        P("row", None),
        P("row", "col"),
        P("col"),
        P("col"),
        P(),
    )
    return jax.shard_map(
        per_device, mesh=mesh, in_specs=placed, out_specs=P("row", "col"), check_vma=False
    )
```

```python
import jax
import jax.numpy as jnp
from jax import lax
from jax.experimental import pallas as pl
from jax.experimental.pallas import tpu as pltpu
from jax.sharding import PartitionSpec as P

SIDE = 4
STEPS = (0, 1, 3, 2)
DEPTH = 3072
LANES = 1024
PART = 384
CHUNK = 192
ROWS = 1024
CAP = 128
QUARTERS = 4
WIDE = LANES // QUARTERS
SET = 2 * WIDE
ROOM = 3
GROUP = SIDE * CAP
CORES = 2
WEIGHTS = ("line", "linepass", "plane", "planepass")
START = (0.0, 6.0, 8.0, 10.0)
RATES = (43.5, 40.0, 400.0)


def plan():
    copies = {}
    for h in range(QUARTERS):
        copies["mirror", h] = ((0, 0, 2, 0), [], 192)
    for g, dy in enumerate(STEPS):
        for dx in (0, 1, 3, 2):
            if dy or dx:
                copies["meta", g, dx] = ((-dy, -dx, 0, 0), [("slot", g)], 4)
                copies["route", g, dx] = ((-dy, -dx, 0, 0), [("slot", g)], 192)
    for h in range(QUARTERS):
        own = [("mirror", h)]
        if h >= 2:
            own += [(kind, h - 2, *j, s) for kind, j in (("line", ()), ("plane", (0,))) for s in (1, -1)]

        def along(axis, step, h=h):
            return (0, step, 0, 0) if axis == h % 2 else (step, 0, 0, 0)

        for s in (1, -1):
            copies["line", h, s] = (along(0, s), own, 192)
            copies["linepass", h, s] = (along(0, s), [("line", h, s)], 96)
        for j in (0, -1, 1, 2):
            if j == 0:
                after = own
            elif j == 2:
                after = [("linepass", h, 1), ("linepass", h, -1)]
            else:
                after = [("line", h, -j)]
            for s in (1, -1):
                copies["plane", h, j, s] = (along(1, s), after, 192)
                copies["planepass", h, j, s] = (along(1, s), [("plane", h, j, s)], 96)
    for g, dy in enumerate(STEPS):
        here = [("slot", g)] + [("route", g, dx) for dx in range(SIDE) if dy or dx]
        copies["own", g] = ((0, 0, 0, 1), here, 768)
        for s in (1, -1):
            copies["ring", g, s] = ((0, 0, s, 0), here, 768)
            copies["ringpass", g, s] = ((0, 0, s, 0), [("ring", g, s)], 384)
            copies["share", g, s] = ((0, 0, 0, 1), [("ring", g, s)], 768)
            copies["sharepass", g, s] = ((0, 0, 0, 1), [("ringpass", g, s)], 384)
    return copies


def schedule(copies):
    free, arrived, issued, order, handled = {}, {}, set(), [], set()
    now = 3.0
    slots_left, units = list(range(SIDE)), []
    for g in range(SIDE):
        units += [(g, half, dz) for half in range(2) for dz in (0, -1, 1, 2)]
    opened, closed = [], []

    def issue(name):
        offset, _, size = copies[name]
        issued.add(name)
        end = now
        for axis, step in enumerate(offset):
            step = (step + 1) % SIDE - 1 if axis < 3 else step
            ways = ((1, 0.5), (-1, 0.5)) if abs(step) == 2 else ((step, 1.0),)
            for way, share in ways:
                if step:
                    link = (axis, way > 0)
                    rate = RATES[2 if axis == 3 else name[0] == "route"]
                    start = max(now, free.get(link, 0.0))
                    free[link] = start + 1.024 * size * share * abs(step) / rate
                    end = max(end, free[link])
        arrived[name] = end + 2.0

    def release():
        for name, (_, after, _) in copies.items():
            if name not in issued and all(n in handled for n in after):
                issue(name)

    release()
    while len(handled) < len(copies) + SIDE or units:
        handled.update(n for n in arrived if n[0] == "meta")
        waiting = sorted((t, str(n), n) for n, t in arrived.items() if n not in handled)
        if slots_left and START[slots_left[0]] <= now:
            g = slots_left.pop(0)
            now += 1.4
            handled.add(("slot", g))
            order.append(("slot", g))
            release()
        elif waiting and waiting[0][0] <= now:
            name = waiting[0][2]
            now += 0.15
            handled.add(name)
            order.append(("wait", name))
            release()
        else:
            unit = None
            for u in units:
                pair = u[:2]
                if pair not in opened and len(opened) >= ROOM and opened[-ROOM] not in closed:
                    continue
                if all(n in handled for n in needs(*u)):
                    unit = u
                    break
            if unit:
                units.remove(unit)
                if unit[:2] not in opened:
                    opened.append(unit[:2])
                if all(u[:2] != unit[:2] for u in units):
                    closed.append(unit[:2])
                now += 1.5
                order.append(("unit", unit))
            else:
                now = min([w[0] for w in waiting[:1]] + [START[g] for g in slots_left[:1]])
    return order


def needs(g, half, dz):
    need = []
    for h in (2 * half, 2 * half + 1):
        need += [("line", h, s) for s in (1, -1)] + [("linepass", h, s) for s in (1, -1)]
        need += [(kind, h, j, s) for kind in ("plane", "planepass") for j in (0, -1, 1, 2) for s in (1, -1)]
    if dz == 0:
        need += [("slot", g), ("own", g)] + [("route", g, dx) for dx in range(SIDE) if STEPS[g] or dx]
    elif dz == 2:
        need += [(kind, g, s) for kind in ("ringpass", "sharepass") for s in (1, -1)]
    else:
        need += [("ring", g, -dz), ("share", g, -dz)]
    return need


def kernel(
    amp, own, gap, irrep, stored, flags, cycle, meta,
    slots, weights, high, low, top_amp, rest_amp, sums, outgoing, mirrored, places, notes, heard, sent, came, done,
):
    row, col = lax.axis_index("row"), lax.axis_index("col")
    y, x, z, k = row // SIDE, row % SIDE, col // CORES, col % CORES

    def device(offset):
        dy, dx, dz, dk = offset
        there = ((y + dy + SIDE) % SIDE) * SIDE + (x + dx + SIDE) % SIDE
        return {"row": there, "col": ((z + dz + SIDE) % SIDE) * CORES + (k + dk) % CORES}

    copies = plan()
    index = {name: i for i, name in enumerate(copies)}
    load = pltpu.make_async_copy(amp, outgoing.at[0 : ROWS // CAP], done.at[ROOM])
    load.start()
    barrier = pltpu.get_barrier_semaphore()
    partners = [(dy, dx, 0, 0) for dy in range(SIDE) for dx in range(SIDE) if dy or dx]
    partners += [(0, 0, 1, 0), (0, 0, 2, 0), (0, 0, 3, 0), (0, 0, 0, 1)]
    for offset in partners:
        pl.semaphore_signal(barrier, inc=1, device_id=device(offset), device_id_type=pl.DeviceIdType.MESH)

    def chunk(h, p, q, part):
        dx, dy = (p, q) if h % 2 == 0 else (q, p)
        at = (((y + dy + SIDE) % SIDE) * SIDE + (x + dx + SIDE) % SIDE) * CHUNK
        size = CHUNK if part == 0 else CHUNK // 2
        at = at + (CHUNK // 2 if part < 0 else 0)
        return pl.ds(pl.multiple_of(at, CHUNK // 2), size), pl.ds(h * WIDE, WIDE)

    def group(dy):
        return ((y + dy) % SIDE) * SIDE

    def held(dz, g, part):
        at = group(STEPS[g]) + (SIDE // 2 if part < 0 else 0)
        size = SIDE if part == 0 else SIDE // 2
        return slots.at[((z + dz + SIDE) % SIDE) * CORES + k, pl.ds(at, size)]

    made = {}

    def copy(name):
        if name in made:
            return made[name]
        kind, rest = name[0], name[1:]
        if kind == "mirror":
            cols = pl.ds(rest[0] * WIDE, WIDE)
            src, dst = stored.at[:, cols], mirrored.at[:, cols]
        elif kind == "meta":
            i = rest[0] * SIDE + rest[1]
            src, dst = notes.at[i], heard.at[row]
        elif kind == "route":
            i = rest[0] * SIDE + rest[1]
            src, dst = outgoing.at[i], slots.at[col, row]
        elif kind in WEIGHTS:
            h, s = rest[0], rest[-1]
            if kind == "line":
                where = chunk(h, 0, 0, 0)
            elif kind == "linepass":
                where = chunk(h, -s, 0, s)
            elif kind == "plane":
                where = chunk(h, rest[1], 0, 0)
            else:
                where = chunk(h, rest[1], -s, s)
            src = dst = weights.at[where]
        else:
            g = rest[0]
            if kind in ("own",):
                src = held(0, g, 0)
            elif kind == "ring":
                src = held(0, g, 0)
            elif kind == "ringpass":
                src = held(-rest[1], g, rest[1])
            elif kind == "share":
                src = held(-rest[1], g, 0)
            else:
                src = held(2, g, rest[1])
            dst = src
        i = index[name]
        made[name] = pltpu.make_async_remote_copy(
            src_ref=src, dst_ref=dst, send_sem=sent.at[i], recv_sem=came.at[i],
            device_id=device(copies[name][0]), device_id_type=pl.DeviceIdType.MESH,
        )
        return made[name]

    def halves(value):
        top = value.astype(jnp.bfloat16)
        return top, (value - top.astype(jnp.float32)).astype(jnp.bfloat16)

    earlier = (
        lax.broadcasted_iota(jnp.int32, (CAP, CAP), 0) < lax.broadcasted_iota(jnp.int32, (CAP, CAP), 1)
    ).astype(jnp.float32).astype(jnp.bfloat16)
    count = jnp.zeros((16, 1), jnp.float32)
    for b in range(ROWS // CAP):
        names = own[:, b * CAP : (b + 1) * CAP]
        hit = lax.broadcasted_iota(jnp.int32, (16, CAP), 0) == names
        one = jnp.where(hit, 1.0, 0.0)
        running = jnp.dot(one.astype(jnp.bfloat16), earlier, preferred_element_type=jnp.float32) + count
        places[:, b * CAP : (b + 1) * CAP] = jnp.where(hit, running, -1.0)
        count = count + jnp.sum(one, axis=1, keepdims=True)

    load.wait()
    top_amp[...], rest_amp[...] = halves(outgoing[0 : ROWS // CAP].reshape(ROWS, PART))
    gap_top, gap_rest = halves(gap[...])
    gap_rest = gap[...] - gap_top.astype(jnp.float32)
    gap_mid, gap_end = halves(gap_rest)
    pieces = [
        gap_top.astype(jnp.float32),
        gap_mid.astype(jnp.float32),
        gap_end.astype(jnp.float32),
        (irrep[...] + 1).astype(jnp.float32),
    ]
    tags = jnp.concatenate(pieces + [jnp.zeros((12, ROWS), jnp.float32)], axis=0).astype(jnp.bfloat16)

    pl.semaphore_wait(barrier, len(partners))
    started = []

    def start(name):
        copy(name).start()
        started.append(name)

    for h in range(QUARTERS):
        start(("mirror", h))

    def slotted(owner):
        place = places[pl.ds(owner, 1), :]
        pick = lax.broadcasted_iota(jnp.int32, (CAP, ROWS), 0).astype(jnp.float32) == place
        pick = jnp.where(pick, 1.0, 0.0).astype(jnp.bfloat16)
        block = jnp.dot(pick, top_amp[...], preferred_element_type=jnp.float32)
        block += jnp.dot(pick, rest_amp[...], preferred_element_type=jnp.float32)
        note = lax.dot_general(tags, pick, (((1,), (1,)), ((), ())), preferred_element_type=jnp.float32)
        return block, note[0:8]

    def slot_group(g):
        for dx in (0, 1, 3, 2):
            there = ((y - STEPS[g] + SIDE) % SIDE) * SIDE + (x - dx + SIDE) % SIDE
            block, note = slotted(there)
            i = g * SIDE + dx
            if i == 0:
                slots[col, row] = block
                heard[row] = note
            else:
                outgoing[i] = block
                notes[i] = note
                start(("route", g, dx))
                start(("meta", g, dx))

    parity = (1 - 2 * flags[col]).astype(jnp.float32)

    def split(where, n):
        rows, cols = where
        first = rows.start

        def body(i, carry):
            at = pl.ds(pl.multiple_of(first + i * 32, 32), 32)
            high[at, cols], low[at, cols] = halves(weights[at, cols])
            return carry

        lax.fori_loop(0, n // 32, body, 0)

    pairs, begun = [], {}

    def write(g, half):
        n = pairs.index((g, half)) % ROOM
        return pltpu.make_async_copy(
            sums.at[n],
            cycle.at[pl.ds(pl.multiple_of(group(STEPS[g]) * CAP, GROUP), GROUP), pl.ds(half * SET, SET)],
            done.at[n],
        )

    def multiply(g, half, dz):
        if (g, half) not in pairs:
            pairs.append((g, half))
            if len(pairs) > ROOM:
                write(*pairs[-1 - ROOM]).wait()
        into = sums.at[pairs.index((g, half)) % ROOM]
        c = (z + dz + SIDE) % SIDE
        both = [
            slots[c * CORES + half, pl.ds(group(STEPS[g]), SIDE)].reshape(GROUP, PART) for half in range(CORES)
        ]
        top, rest = halves(jnp.concatenate(both, axis=1))
        at = pl.ds(pl.multiple_of(c * (CORES * PART), CORES * PART), CORES * PART)
        for n in range(0, SET, 256):
            cols = pl.ds(half * SET + n, 256)
            w = high[at, cols]
            add = jnp.dot(top, w, preferred_element_type=jnp.float32)
            add += jnp.dot(rest, w, preferred_element_type=jnp.float32)
            add += jnp.dot(top, low[at, cols], preferred_element_type=jnp.float32)
            if (g, half) in begun:
                into[:, n : n + 256] += add
            else:
                into[:, n : n + 256] = add
        begun[g, half] = begun.get((g, half), 0) + 1
        if begun[g, half] == SIDE:
            write(g, half).start()

    seen = set()

    def follow(name):
        seen.add(name)
        for other, (_, after, _) in copies.items():
            if other not in started and name in after and all(n in seen for n in after):
                start(other)

    for act, name in schedule(copies):
        if act == "unit":
            multiply(*name)
            continue
        if act == "slot":
            slot_group(name)
            follow((act, name))
            continue
        copy(name).wait_recv()
        kind = name[0]
        if kind == "mirror":
            cols = pl.ds(name[1] * WIDE, WIDE)
            mine = chunk(name[1], 0, 0, 0)
            weights[mine] = stored[:, cols] + parity * mirrored[:, cols]
        follow(name)
        if kind == "mirror":
            split(mine, CHUNK)
        if kind in WEIGHTS:
            h, s = name[1], name[-1]
            if kind == "line":
                split(chunk(h, -s, 0, 0), CHUNK)
            elif kind == "linepass":
                split(chunk(h, -2 * s, 0, s), CHUNK // 2)
            elif kind == "plane":
                split(chunk(h, name[2], -s, 0), CHUNK)
            else:
                split(chunk(h, name[2], -2 * s, s), CHUNK // 2)

    for n in copies:
        if n[0] == "meta":
            copy(n).wait_recv()
    for i in range(16):
        meta[i] = heard[i]
    for n in copies:
        copy(n).wait_send()
    for pair in pairs[-ROOM:]:
        write(*pair).wait()


def exchange(amp, own, gap, irrep, stored, flags):
    n = len(plan())
    vmem = pl.BlockSpec(memory_space=pltpu.VMEM)
    return pl.pallas_call(
        kernel,
        out_shape=(
            jax.ShapeDtypeStruct((16 * CAP, LANES), jnp.float32),
            jax.ShapeDtypeStruct((16, 8, CAP), jnp.float32),
        ),
        in_specs=[pl.BlockSpec(memory_space=pl.ANY)] + [vmem] * 4 + [pl.BlockSpec(memory_space=pltpu.SMEM)],
        out_specs=(pl.BlockSpec(memory_space=pl.ANY), vmem),
        scratch_shapes=[
            pltpu.VMEM((SIDE * CORES, 16, CAP, PART), jnp.float32),
            pltpu.VMEM((DEPTH, LANES), jnp.float32),
            pltpu.VMEM((DEPTH, LANES), jnp.bfloat16),
            pltpu.VMEM((DEPTH, LANES), jnp.bfloat16),
            pltpu.VMEM((ROWS, PART), jnp.bfloat16),
            pltpu.VMEM((ROWS, PART), jnp.bfloat16),
            pltpu.VMEM((ROOM, GROUP, SET), jnp.float32),
            pltpu.VMEM((16, CAP, PART), jnp.float32),
            pltpu.VMEM((CHUNK, LANES), jnp.float32),
            pltpu.VMEM((16, ROWS), jnp.float32),
            pltpu.VMEM((16, 8, CAP), jnp.float32),
            pltpu.VMEM((16, 8, CAP), jnp.float32),
            pltpu.SemaphoreType.DMA((n,)),
            pltpu.SemaphoreType.DMA((n,)),
            pltpu.SemaphoreType.DMA((ROOM + 1,)),
        ],
        compiler_params=pltpu.CompilerParams(
            collective_id=0, has_side_effects=True, vmem_limit_bytes=60 * 2**20
        ),
        name="exchange",
    )(amp, own, gap, irrep, stored, flags)


def per_device(amplitudes, row_gap, row_irrep, owners, stored, col_gap, col_irrep, mirror_flags):
    line = (1, ROWS)
    cycle, meta = exchange(
        amplitudes.reshape(ROWS // CAP, CAP, PART), owners.reshape(line), row_gap.reshape(line), row_irrep.reshape(line), stored, mirror_flags
    )
    gap = (meta[:, 0] + meta[:, 1] + meta[:, 2]).reshape(-1, 1)
    irrep = (meta[:, 3] - 1.0).reshape(-1, 1)
    same = irrep == col_irrep.astype(jnp.float32)[None, :]
    return jnp.where(same, cycle / (gap + col_gap[None, :]), 0.0)


def solution(mesh):
    placed = (
        P("row", "col"),
        P("row"),
        P("row"),
        P("row", None),
        P("row", "col"),
        P("col"),
        P("col"),
        P(),
    )
    return jax.shard_map(
        per_device, mesh=mesh, in_specs=placed, out_specs=P("row", "col"), check_vma=False
    )
```

```python
import jax
import jax.numpy as jnp
from jax import lax
from jax.experimental import pallas as pl
from jax.experimental.pallas import tpu as pltpu
from jax.sharding import PartitionSpec as P

SIDE = 4
STEPS = (0, 1, 3, 2)
DEPTH = 3072
LANES = 1024
PART = 384
CHUNK = 192
ROWS = 1024
CAP = 128
WIDTHS = (512, 512)
FROM = (0, 512)
TILE = 256
TILES = LANES // TILE
PIECES = 2 * len(WIDTHS)
GROUP = SIDE * CAP
CORES = 2
WEIGHTS = ("line", "linepass", "plane", "planepass")
START = (0.0, 6.0, 8.0, 10.0)
RATES = (45.0, 55.0, 400.0)


def wide(h):
    return WIDTHS[h // 2] // 2


def columns(h):
    return FROM[h // 2] + h % 2 * wide(h)


def plan():
    copies = {}
    for h in range(PIECES):
        copies["mirror", h] = ((0, 0, 2, 0), [], wide(h) * 3 // 4)
    for g, dy in enumerate(STEPS):
        for dx in (0, 1, 3, 2):
            if dy or dx:
                copies["meta", g, dx] = ((-dy, -dx, 0, 0), [("slot", g)], 4)
                copies["route", g, dx] = ((-dy, -dx, 0, 0), [("slot", g)], 192)
    for h in range(PIECES):
        own, size = [("mirror", h)], wide(h) * 3 // 4
        if h >= 2:
            own += [(kind, h - 2, *j, s) for kind, j in (("line", ()), ("plane", (0,))) for s in (1, -1)]

        def along(axis, step, h=h):
            return (0, step, 0, 0) if axis == h % 2 else (step, 0, 0, 0)

        for s in (1, -1):
            copies["line", h, s] = (along(0, s), own, size)
            copies["linepass", h, s] = (along(0, s), [("line", h, s)], size / 2)
        for j in (0, -1, 1, 2):
            if j == 0:
                after = own
            elif j == 2:
                after = [("linepass", h, 1), ("linepass", h, -1)]
            else:
                after = [("line", h, -j)]
            for s in (1, -1):
                copies["plane", h, j, s] = (along(1, s), after, size)
                copies["planepass", h, j, s] = (along(1, s), [("plane", h, j, s)], size / 2)
    for g, dy in enumerate(STEPS):
        here = [("slot", g)] + [("route", g, dx) for dx in range(SIDE) if dy or dx]
        copies["own", g] = ((0, 0, 0, 1), here, 768)
        for s in (1, -1):
            pace = [("ring", g - 2, s)] if g >= 2 else []
            copies["ring", g, s] = ((0, 0, s, 0), here + pace, 768)
            copies["ringpass", g, s] = ((0, 0, s, 0), [("ring", g, s)], 384)
            copies["share", g, s] = ((0, 0, 0, 1), [("ring", g, s)], 768)
            copies["sharepass", g, s] = ((0, 0, 0, 1), [("ringpass", g, s)], 384)
    return copies


def schedule(copies):
    free, arrived, issued, order, handled = {}, {}, set(), [], set()
    now = 3.0
    slots_left, units = list(range(SIDE)), []
    for g in range(SIDE):
        units += [(g, n, dz) for n in range(len(WIDTHS)) for dz in (0, -1, 1, 2)]

    def issue(name):
        offset, _, size = copies[name]
        issued.add(name)
        end = now
        for axis, step in enumerate(offset):
            step = (step + 1) % SIDE - 1 if axis < 3 else step
            ways = ((1, 0.5), (-1, 0.5)) if abs(step) == 2 else ((step, 1.0),)
            for way, share in ways:
                if step:
                    link = (axis, way > 0)
                    rate = RATES[2 if axis == 3 else name[0] == "route"]
                    start = max(now, free.get(link, 0.0))
                    free[link] = start + 1.024 * size * share * abs(step) / rate
                    end = max(end, free[link])
        arrived[name] = end + 2.0

    def release():
        for name, (_, after, _) in copies.items():
            if name not in issued and all(n in handled for n in after):
                issue(name)

    release()
    while len(handled) < len(copies) + SIDE or units:
        handled.update(n for n in arrived if n[0] == "meta")
        waiting = sorted((t, str(n), n) for n, t in arrived.items() if n not in handled)
        if slots_left and START[slots_left[0]] <= now:
            g = slots_left.pop(0)
            now += 1.4
            handled.add(("slot", g))
            order.append(("slot", g))
            release()
        elif waiting and waiting[0][0] <= now:
            name = waiting[0][2]
            now += 0.15
            handled.add(name)
            order.append(("wait", name))
            release()
        else:
            unit = None
            for u in units:
                if all(n in handled for n in needs(*u)):
                    unit = u
                    break
            if unit:
                units.remove(unit)
                now += 2.8 * WIDTHS[unit[1]] / LANES
                order.append(("unit", unit))
            else:
                now = min([w[0] for w in waiting[:1]] + [START[g] for g in slots_left[:1]])
    return order


def needs(g, n, dz):
    need = []
    for h in (0, 1, 2 * n, 2 * n + 1):
        need += [("line", h, s) for s in (1, -1)] + [("linepass", h, s) for s in (1, -1)]
        need += [(kind, h, j, s) for kind in ("plane", "planepass") for j in (0, -1, 1, 2) for s in (1, -1)]
    if dz == 0:
        need += [("slot", g), ("own", g)] + [("route", g, dx) for dx in range(SIDE) if STEPS[g] or dx]
    elif dz == 2:
        need += [(kind, g, s) for kind in ("ringpass", "sharepass") for s in (1, -1)]
    else:
        need += [("ring", g, -dz), ("share", g, -dz)]
    return need


def kernel(
    amp, own, gap, irrep, stored, flags, cycle, meta,
    slots, weights, high, low, top_amp, rest_amp, sums, outgoing, mirrored, places, notes, heard, sent, came, done,
):
    row, col = lax.axis_index("row"), lax.axis_index("col")
    y, x, z, k = row // SIDE, row % SIDE, col // CORES, col % CORES

    def device(offset):
        dy, dx, dz, dk = offset
        there = ((y + dy + SIDE) % SIDE) * SIDE + (x + dx + SIDE) % SIDE
        return {"row": there, "col": ((z + dz + SIDE) % SIDE) * CORES + (k + dk) % CORES}

    copies = plan()
    index = {name: i for i, name in enumerate(copies)}
    load = pltpu.make_async_copy(amp, outgoing.at[0 : ROWS // CAP], done.at[SIDE * TILES])
    load.start()
    barrier = pltpu.get_barrier_semaphore()
    partners = [(dy, dx, 0, 0) for dy in range(SIDE) for dx in range(SIDE) if dy or dx]
    partners += [(0, 0, 1, 0), (0, 0, 2, 0), (0, 0, 3, 0), (0, 0, 0, 1)]
    for offset in partners:
        pl.semaphore_signal(barrier, inc=1, device_id=device(offset), device_id_type=pl.DeviceIdType.MESH)

    def chunk(h, p, q, part):
        dx, dy = (p, q) if h % 2 == 0 else (q, p)
        at = (((y + dy + SIDE) % SIDE) * SIDE + (x + dx + SIDE) % SIDE) * CHUNK
        size = CHUNK if part == 0 else CHUNK // 2
        at = at + (CHUNK // 2 if part < 0 else 0)
        return h, pl.ds(pl.multiple_of(at, CHUNK // 2), size)

    def group(dy):
        return ((y + dy) % SIDE) * SIDE

    def held(dz, g, part):
        at = group(STEPS[g]) + (SIDE // 2 if part < 0 else 0)
        size = SIDE if part == 0 else SIDE // 2
        return slots.at[((z + dz + SIDE) % SIDE) * CORES + k, pl.ds(at, size)]

    made = {}

    def copy(name):
        if name in made:
            return made[name]
        kind, rest = name[0], name[1:]
        if kind == "mirror":
            src, dst = stored.at[:, pl.ds(columns(rest[0]), wide(rest[0]))], mirrored.at[rest[0]]
        elif kind == "meta":
            i = rest[0] * SIDE + rest[1]
            src, dst = notes.at[i], heard.at[row]
        elif kind == "route":
            i = rest[0] * SIDE + rest[1]
            src, dst = outgoing.at[i], slots.at[col, row]
        elif kind in WEIGHTS:
            h, s = rest[0], rest[-1]
            if kind == "line":
                where = chunk(h, 0, 0, 0)
            elif kind == "linepass":
                where = chunk(h, -s, 0, s)
            elif kind == "plane":
                where = chunk(h, rest[1], 0, 0)
            else:
                where = chunk(h, rest[1], -s, s)
            src = dst = weights.at[where]
        else:
            g = rest[0]
            if kind in ("own",):
                src = held(0, g, 0)
            elif kind == "ring":
                src = held(0, g, 0)
            elif kind == "ringpass":
                src = held(-rest[1], g, rest[1])
            elif kind == "share":
                src = held(-rest[1], g, 0)
            else:
                src = held(2, g, rest[1])
            dst = src
        i = index[name]
        made[name] = pltpu.make_async_remote_copy(
            src_ref=src, dst_ref=dst, send_sem=sent.at[i], recv_sem=came.at[i],
            device_id=device(copies[name][0]), device_id_type=pl.DeviceIdType.MESH,
        )
        return made[name]

    def halves(value):
        top = value.astype(jnp.bfloat16)
        return top, (value - top.astype(jnp.float32)).astype(jnp.bfloat16)

    earlier = (
        lax.broadcasted_iota(jnp.int32, (CAP, CAP), 0) < lax.broadcasted_iota(jnp.int32, (CAP, CAP), 1)
    ).astype(jnp.float32).astype(jnp.bfloat16)
    count = jnp.zeros((16, 1), jnp.float32)
    for b in range(ROWS // CAP):
        names = own[:, b * CAP : (b + 1) * CAP]
        hit = lax.broadcasted_iota(jnp.int32, (16, CAP), 0) == names
        one = jnp.where(hit, 1.0, 0.0)
        running = jnp.dot(one.astype(jnp.bfloat16), earlier, preferred_element_type=jnp.float32) + count
        places[:, b * CAP : (b + 1) * CAP] = jnp.where(hit, running, -1.0)
        count = count + jnp.sum(one, axis=1, keepdims=True)

    load.wait()
    top_amp[...], rest_amp[...] = halves(outgoing[0 : ROWS // CAP].reshape(ROWS, PART))
    gap_top, gap_rest = halves(gap[...])
    gap_rest = gap[...] - gap_top.astype(jnp.float32)
    gap_mid, gap_end = halves(gap_rest)
    pieces = [
        gap_top.astype(jnp.float32),
        gap_mid.astype(jnp.float32),
        gap_end.astype(jnp.float32),
        (irrep[...] + 1).astype(jnp.float32),
    ]
    tags = jnp.concatenate(pieces + [jnp.zeros((12, ROWS), jnp.float32)], axis=0).astype(jnp.bfloat16)

    pl.semaphore_wait(barrier, len(partners))
    started = []

    def start(name):
        copy(name).start()
        started.append(name)

    for h in range(PIECES):
        start(("mirror", h))

    def slotted(owner):
        place = places[pl.ds(owner, 1), :]
        pick = lax.broadcasted_iota(jnp.int32, (CAP, ROWS), 0).astype(jnp.float32) == place
        pick = jnp.where(pick, 1.0, 0.0).astype(jnp.bfloat16)
        block = jnp.dot(pick, top_amp[...], preferred_element_type=jnp.float32)
        block += jnp.dot(pick, rest_amp[...], preferred_element_type=jnp.float32)
        note = lax.dot_general(tags, pick, (((1,), (1,)), ((), ())), preferred_element_type=jnp.float32)
        return block, note[0:8]

    def slot_group(g):
        for dx in (0, 1, 3, 2):
            there = ((y - STEPS[g] + SIDE) % SIDE) * SIDE + (x - dx + SIDE) % SIDE
            block, note = slotted(there)
            i = g * SIDE + dx
            if i == 0:
                slots[col, row] = block
                heard[row] = note
            else:
                outgoing[i] = block
                notes[i] = note
                start(("route", g, dx))
                start(("meta", g, dx))

    parity = (1 - 2 * flags[col]).astype(jnp.float32)

    def split(where, n):
        h, rows = where
        first, cols = rows.start, pl.ds(columns(h), wide(h))

        def body(i, carry):
            at = pl.ds(pl.multiple_of(first + i * 32, 32), 32)
            high[at, cols], low[at, cols] = halves(weights[h, at])
            return carry

        lax.fori_loop(0, n // 32, body, 0)

    begun = {}

    def total(g, m):
        if g == SIDE - 1:
            return sums.at[m]
        block = g * TILES + m
        return weights.at[block // 6, pl.ds(block % 6 * GROUP, GROUP)]

    def write(g, m):
        at = pl.ds(pl.multiple_of(group(STEPS[g]) * CAP, GROUP), GROUP)
        return pltpu.make_async_copy(total(g, m), cycle.at[at, pl.ds(m * TILE, TILE)], done.at[g * TILES + m])

    def multiply(g, n, dz):
        c = (z + dz + SIDE) % SIDE
        both = [slots[c * CORES + i, pl.ds(group(STEPS[g]), SIDE)].reshape(GROUP, PART) for i in range(CORES)]
        top, rest = halves(jnp.concatenate(both, axis=1))
        at = pl.ds(pl.multiple_of(c * (CORES * PART), CORES * PART), CORES * PART)
        begun[g, n] = begun.get((g, n), 0) + 1
        for m in range(FROM[n] // TILE, (FROM[n] + WIDTHS[n]) // TILE):
            cols = pl.ds(m * TILE, TILE)
            w = high[at, cols]
            add = jnp.dot(top, w, preferred_element_type=jnp.float32)
            add += jnp.dot(rest, w, preferred_element_type=jnp.float32)
            add += jnp.dot(top, low[at, cols], preferred_element_type=jnp.float32)
            into = total(g, m)
            if begun[g, n] > 1:
                into[...] += add
            else:
                into[...] = add
            if begun[g, n] == SIDE:
                write(g, m).start()

    seen = set()
    first_left = sum(n[0] in WEIGHTS and n[1] < 2 for n in copies)

    def follow(name):
        seen.add(name)
        for other, (_, after, _) in copies.items():
            if other not in started and name in after and all(n in seen for n in after):
                start(other)

    for act, name in schedule(copies):
        if act == "unit":
            multiply(*name)
            continue
        if act == "slot":
            slot_group(name)
            follow((act, name))
            continue
        copy(name).wait_recv()
        kind = name[0]
        if kind == "mirror":
            cols = pl.ds(columns(name[1]), wide(name[1]))
            mine = chunk(name[1], 0, 0, 0)
            weights[mine] = stored[:, cols] + parity * mirrored[name[1]]
        follow(name)
        if kind == "mirror":
            split(mine, CHUNK)
        if kind in WEIGHTS:
            h, s = name[1], name[-1]
            if kind == "line":
                split(chunk(h, -s, 0, 0), CHUNK)
            elif kind == "linepass":
                split(chunk(h, -2 * s, 0, s), CHUNK // 2)
            elif kind == "plane":
                split(chunk(h, name[2], -s, 0), CHUNK)
            else:
                split(chunk(h, name[2], -2 * s, s), CHUNK // 2)
            if h < 2:
                first_left -= 1
                if first_left == 0:
                    for n in copies:
                        if n[0] in WEIGHTS and n[1] < 2:
                            copy(n).wait_send()

    for n in copies:
        if n[0] == "meta":
            copy(n).wait_recv()
    for i in range(16):
        meta[i] = heard[i]
    for n in copies:
        if n[0] not in WEIGHTS or n[1] >= 2:
            copy(n).wait_send()
    for g in range(SIDE):
        for m in range(TILES):
            write(g, m).wait()


def exchange(amp, own, gap, irrep, stored, flags):
    n = len(plan())
    vmem = pl.BlockSpec(memory_space=pltpu.VMEM)
    return pl.pallas_call(
        kernel,
        out_shape=(
            jax.ShapeDtypeStruct((16 * CAP, LANES), jnp.float32),
            jax.ShapeDtypeStruct((16, 8, CAP), jnp.float32),
        ),
        in_specs=[pl.BlockSpec(memory_space=pl.ANY)] + [vmem] * 4 + [pl.BlockSpec(memory_space=pltpu.SMEM)],
        out_specs=(pl.BlockSpec(memory_space=pl.ANY), vmem),
        scratch_shapes=[
            pltpu.VMEM((SIDE * CORES, 16, CAP, PART), jnp.float32),
            pltpu.VMEM((PIECES, DEPTH, TILE), jnp.float32),
            pltpu.VMEM((DEPTH, LANES), jnp.bfloat16),
            pltpu.VMEM((DEPTH, LANES), jnp.bfloat16),
            pltpu.VMEM((ROWS, PART), jnp.bfloat16),
            pltpu.VMEM((ROWS, PART), jnp.bfloat16),
            pltpu.VMEM((TILES, GROUP, TILE), jnp.float32),
            pltpu.VMEM((16, CAP, PART), jnp.float32),
            pltpu.VMEM((PIECES, CHUNK, TILE), jnp.float32),
            pltpu.VMEM((16, ROWS), jnp.float32),
            pltpu.VMEM((16, 8, CAP), jnp.float32),
            pltpu.VMEM((16, 8, CAP), jnp.float32),
            pltpu.SemaphoreType.DMA((n,)),
            pltpu.SemaphoreType.DMA((n,)),
            pltpu.SemaphoreType.DMA((SIDE * TILES + 1,)),
        ],
        compiler_params=pltpu.CompilerParams(
            collective_id=0, has_side_effects=True, vmem_limit_bytes=60 * 2**20
        ),
        name="exchange",
    )(amp, own, gap, irrep, stored, flags)


def per_device(amplitudes, row_gap, row_irrep, owners, stored, col_gap, col_irrep, mirror_flags):
    line = (1, ROWS)
    cycle, meta = exchange(
        amplitudes.reshape(ROWS // CAP, CAP, PART), owners.reshape(line), row_gap.reshape(line), row_irrep.reshape(line), stored, mirror_flags
    )
    gap = (meta[:, 0] + meta[:, 1] + meta[:, 2]).reshape(-1, 1)
    irrep = (meta[:, 3] - 1.0).reshape(-1, 1)
    same = irrep == col_irrep.astype(jnp.float32)[None, :]
    return jnp.where(same, cycle / (gap + col_gap[None, :]), 0.0)


def solution(mesh):
    placed = (
        P("row", "col"),
        P("row"),
        P("row"),
        P("row", None),
        P("row", "col"),
        P("col"),
        P("col"),
        P(),
    )
    return jax.shard_map(
        per_device, mesh=mesh, in_specs=placed, out_specs=P("row", "col"), check_vma=False
    )
```

```python
import jax
import jax.numpy as jnp
from jax import lax
from jax.experimental import pallas as pl
from jax.experimental.pallas import tpu as pltpu
from jax.sharding import PartitionSpec as P

SIDE = 4
STEPS = (0, 1, 3, 2)
DEPTH = 3072
LANES = 1024
PART = 384
CHUNK = 192
ROWS = 1024
CAP = 128
WIDTHS = (512, 512)
FROM = (0, 512)
TILE = 256
TILES = LANES // TILE
PIECES = 2 * len(WIDTHS)
GROUP = SIDE * CAP
CORES = 2
WEIGHTS = ("line", "linepass", "plane", "planepass")
START = (0.0, 6.0, 8.0, 50.0)
RATES = (45.0, 55.0, 400.0)


def wide(h):
    return WIDTHS[h // 2] // 2


def columns(h):
    return FROM[h // 2] + h % 2 * wide(h)


def plan():
    copies = {}
    for h in range(PIECES):
        copies["mirror", h] = ((0, 0, 2, 0), [], wide(h) * 3 // 4)
    for g, dy in enumerate(STEPS):
        for dx in (0, 1, 3, 2):
            if dy or dx:
                copies["meta", g, dx] = ((-dy, -dx, 0, 0), [("slot", g)], 4)
                copies["route", g, dx] = ((-dy, -dx, 0, 0), [("slot", g)], 192)
    for h in range(PIECES):
        own, size = [("mirror", h)], wide(h) * 3 // 4
        if h >= 2:
            own += [("linepass", h - 2, 1), ("linepass", h - 2, -1)]

        def along(axis, step, h=h):
            return (0, step, 0, 0) if axis == h % 2 else (step, 0, 0, 0)

        for s in (1, -1):
            copies["line", h, s] = (along(0, s), own, size)
            copies["linepass", h, s] = (along(0, s), [("line", h, s)], size / 2)
        for j in (0, -1, 1, 2):
            if j == 0:
                after = own
            elif j == 2:
                after = [("linepass", h, 1), ("linepass", h, -1)]
            else:
                after = [("line", h, -j)]
            for s in (1, -1):
                copies["plane", h, j, s] = (along(1, s), after, size)
                copies["planepass", h, j, s] = (along(1, s), [("plane", h, j, s)], size / 2)
    for g, dy in enumerate(STEPS):
        here = [("slot", g)] + [("route", g, dx) for dx in range(SIDE) if dy or dx]
        copies["own", g] = ((0, 0, 0, 1), here, 768)
        for s in (1, -1):
            pace = [("ring", g - 2, s)] if g >= 2 else []
            copies["ring", g, s] = ((0, 0, s, 0), here + pace, 768)
            copies["ringpass", g, s] = ((0, 0, s, 0), [("ring", g, s)], 384)
            copies["share", g, s] = ((0, 0, 0, 1), [("ring", g, s)], 768)
            copies["sharepass", g, s] = ((0, 0, 0, 1), [("ringpass", g, s)], 384)
    return copies


def schedule(copies):
    free, arrived, issued, order, handled = {}, {}, set(), [], set()
    now = 3.0
    slots_left, units = list(range(SIDE)), []
    for g in range(SIDE):
        units += [(g, n, dz) for n in range(len(WIDTHS)) for dz in (0, -1, 1, 2)]

    def issue(name):
        offset, _, size = copies[name]
        issued.add(name)
        end = now
        for axis, step in enumerate(offset):
            step = (step + 1) % SIDE - 1 if axis < 3 else step
            ways = ((1, 0.5), (-1, 0.5)) if abs(step) == 2 else ((step, 1.0),)
            for way, share in ways:
                if step:
                    link = (axis, way > 0)
                    rate = RATES[2 if axis == 3 else name[0] == "route"]
                    start = max(now, free.get(link, 0.0))
                    free[link] = start + 1.024 * size * share * abs(step) / rate
                    end = max(end, free[link])
        arrived[name] = end + 2.0

    def release():
        for name, (_, after, _) in copies.items():
            if name not in issued and all(n in handled for n in after):
                issue(name)

    release()
    while len(handled) < len(copies) + SIDE or units:
        handled.update(n for n in arrived if n[0] == "meta")
        waiting = sorted((t, str(n), n) for n, t in arrived.items() if n not in handled)
        if slots_left and START[slots_left[0]] <= now:
            g = slots_left.pop(0)
            now += 1.4
            handled.add(("slot", g))
            order.append(("slot", g))
            release()
        elif waiting and waiting[0][0] <= now:
            name = waiting[0][2]
            now += 0.15
            handled.add(name)
            order.append(("wait", name))
            release()
        else:
            unit = None
            for u in units:
                if all(n in handled for n in needs(*u)):
                    unit = u
                    break
            if unit:
                units.remove(unit)
                now += 2.8 * WIDTHS[unit[1]] / LANES
                order.append(("unit", unit))
            else:
                now = min([w[0] for w in waiting[:1]] + [START[g] for g in slots_left[:1]])
    return order


def needs(g, n, dz):
    need = []
    for h in (0, 1, 2 * n, 2 * n + 1):
        need += [("line", h, s) for s in (1, -1)] + [("linepass", h, s) for s in (1, -1)]
        need += [(kind, h, j, s) for kind in ("plane", "planepass") for j in (0, -1, 1, 2) for s in (1, -1)]
    if dz == 0:
        need += [("slot", g), ("own", g)] + [("route", g, dx) for dx in range(SIDE) if STEPS[g] or dx]
    elif dz == 2:
        need += [(kind, g, s) for kind in ("ringpass", "sharepass") for s in (1, -1)]
    else:
        need += [("ring", g, -dz), ("share", g, -dz)]
    return need


def kernel(
    amp, own, gap, irrep, stored, flags, cycle, meta,
    slots, weights, high, low, top_amp, rest_amp, sums, outgoing, mirrored, places, notes, heard, sent, came, done,
):
    row, col = lax.axis_index("row"), lax.axis_index("col")
    y, x, z, k = row // SIDE, row % SIDE, col // CORES, col % CORES

    def device(offset):
        dy, dx, dz, dk = offset
        there = ((y + dy + SIDE) % SIDE) * SIDE + (x + dx + SIDE) % SIDE
        return {"row": there, "col": ((z + dz + SIDE) % SIDE) * CORES + (k + dk) % CORES}

    copies = plan()
    index = {name: i for i, name in enumerate(copies)}
    load = pltpu.make_async_copy(amp, outgoing.at[0 : ROWS // CAP], done.at[SIDE * TILES])
    load.start()
    barrier = pltpu.get_barrier_semaphore()
    partners = [(dy, dx, 0, 0) for dy in range(SIDE) for dx in range(SIDE) if dy or dx]
    partners += [(0, 0, 1, 0), (0, 0, 2, 0), (0, 0, 3, 0), (0, 0, 0, 1)]
    for offset in partners:
        pl.semaphore_signal(barrier, inc=1, device_id=device(offset), device_id_type=pl.DeviceIdType.MESH)

    def chunk(h, p, q, part):
        dx, dy = (p, q) if h % 2 == 0 else (q, p)
        at = (((y + dy + SIDE) % SIDE) * SIDE + (x + dx + SIDE) % SIDE) * CHUNK
        size = CHUNK if part == 0 else CHUNK // 2
        at = at + (CHUNK // 2 if part < 0 else 0)
        return h, pl.ds(pl.multiple_of(at, CHUNK // 2), size)

    def group(dy):
        return ((y + dy) % SIDE) * SIDE

    def held(dz, g, part):
        at = group(STEPS[g]) + (SIDE // 2 if part < 0 else 0)
        size = SIDE if part == 0 else SIDE // 2
        return slots.at[((z + dz + SIDE) % SIDE) * CORES + k, pl.ds(at, size)]

    made = {}

    def copy(name):
        if name in made:
            return made[name]
        kind, rest = name[0], name[1:]
        if kind == "mirror":
            src, dst = stored.at[:, pl.ds(columns(rest[0]), wide(rest[0]))], mirrored.at[rest[0]]
        elif kind == "meta":
            i = rest[0] * SIDE + rest[1]
            src, dst = notes.at[i], heard.at[row]
        elif kind == "route":
            i = rest[0] * SIDE + rest[1]
            src, dst = outgoing.at[i], slots.at[col, row]
        elif kind in WEIGHTS:
            h, s = rest[0], rest[-1]
            if kind == "line":
                where = chunk(h, 0, 0, 0)
            elif kind == "linepass":
                where = chunk(h, -s, 0, s)
            elif kind == "plane":
                where = chunk(h, rest[1], 0, 0)
            else:
                where = chunk(h, rest[1], -s, s)
            src = dst = weights.at[where]
        else:
            g = rest[0]
            if kind in ("own",):
                src = held(0, g, 0)
            elif kind == "ring":
                src = held(0, g, 0)
            elif kind == "ringpass":
                src = held(-rest[1], g, rest[1])
            elif kind == "share":
                src = held(-rest[1], g, 0)
            else:
                src = held(2, g, rest[1])
            dst = src
        i = index[name]
        made[name] = pltpu.make_async_remote_copy(
            src_ref=src, dst_ref=dst, send_sem=sent.at[i], recv_sem=came.at[i],
            device_id=device(copies[name][0]), device_id_type=pl.DeviceIdType.MESH,
        )
        return made[name]

    def halves(value):
        top = value.astype(jnp.bfloat16)
        return top, (value - top.astype(jnp.float32)).astype(jnp.bfloat16)

    earlier = (
        lax.broadcasted_iota(jnp.int32, (CAP, CAP), 0) < lax.broadcasted_iota(jnp.int32, (CAP, CAP), 1)
    ).astype(jnp.float32).astype(jnp.bfloat16)
    count = jnp.zeros((16, 1), jnp.float32)
    for b in range(ROWS // CAP):
        names = own[:, b * CAP : (b + 1) * CAP]
        hit = lax.broadcasted_iota(jnp.int32, (16, CAP), 0) == names
        one = jnp.where(hit, 1.0, 0.0)
        running = jnp.dot(one.astype(jnp.bfloat16), earlier, preferred_element_type=jnp.float32) + count
        places[:, b * CAP : (b + 1) * CAP] = jnp.where(hit, running, -1.0)
        count = count + jnp.sum(one, axis=1, keepdims=True)

    load.wait()
    top_amp[...], rest_amp[...] = halves(outgoing[0 : ROWS // CAP].reshape(ROWS, PART))
    gap_top, gap_rest = halves(gap[...])
    gap_rest = gap[...] - gap_top.astype(jnp.float32)
    gap_mid, gap_end = halves(gap_rest)
    pieces = [
        gap_top.astype(jnp.float32),
        gap_mid.astype(jnp.float32),
        gap_end.astype(jnp.float32),
        (irrep[...] + 1).astype(jnp.float32),
    ]
    tags = jnp.concatenate(pieces + [jnp.zeros((12, ROWS), jnp.float32)], axis=0).astype(jnp.bfloat16)

    pl.semaphore_wait(barrier, len(partners))
    started = []

    def start(name):
        copy(name).start()
        started.append(name)

    for h in range(PIECES):
        start(("mirror", h))

    def slotted(owner):
        place = places[pl.ds(owner, 1), :]
        pick = lax.broadcasted_iota(jnp.int32, (CAP, ROWS), 0).astype(jnp.float32) == place
        pick = jnp.where(pick, 1.0, 0.0).astype(jnp.bfloat16)
        block = jnp.dot(pick, top_amp[...], preferred_element_type=jnp.float32)
        block += jnp.dot(pick, rest_amp[...], preferred_element_type=jnp.float32)
        note = lax.dot_general(tags, pick, (((1,), (1,)), ((), ())), preferred_element_type=jnp.float32)
        return block, note[0:8]

    def slot_group(g):
        for dx in (0, 1, 3, 2):
            there = ((y - STEPS[g] + SIDE) % SIDE) * SIDE + (x - dx + SIDE) % SIDE
            block, note = slotted(there)
            i = g * SIDE + dx
            if i == 0:
                slots[col, row] = block
                heard[row] = note
            else:
                outgoing[i] = block
                notes[i] = note
                start(("route", g, dx))
                start(("meta", g, dx))

    parity = (1 - 2 * flags[col]).astype(jnp.float32)

    def split(where, n):
        h, rows = where
        first, cols = rows.start, pl.ds(columns(h), wide(h))

        def body(i, carry):
            at = pl.ds(pl.multiple_of(first + i * 32, 32), 32)
            high[at, cols], low[at, cols] = halves(weights[h, at])
            return carry

        lax.fori_loop(0, n // 32, body, 0)

    begun = {}

    def total(g, m):
        if g == SIDE - 1:
            return sums.at[m]
        block = g * TILES + m
        return weights.at[block // 6, pl.ds(block % 6 * GROUP, GROUP)]

    def write(g, m):
        at = pl.ds(pl.multiple_of(group(STEPS[g]) * CAP, GROUP), GROUP)
        return pltpu.make_async_copy(total(g, m), cycle.at[at, pl.ds(m * TILE, TILE)], done.at[g * TILES + m])

    def multiply(g, n, dz):
        c = (z + dz + SIDE) % SIDE
        both = [slots[c * CORES + i, pl.ds(group(STEPS[g]), SIDE)].reshape(GROUP, PART) for i in range(CORES)]
        top, rest = halves(jnp.concatenate(both, axis=1))
        at = pl.ds(pl.multiple_of(c * (CORES * PART), CORES * PART), CORES * PART)
        begun[g, n] = begun.get((g, n), 0) + 1
        for m in range(FROM[n] // TILE, (FROM[n] + WIDTHS[n]) // TILE):
            cols = pl.ds(m * TILE, TILE)
            w = high[at, cols]
            add = jnp.dot(top, w, preferred_element_type=jnp.float32)
            add += jnp.dot(rest, w, preferred_element_type=jnp.float32)
            add += jnp.dot(top, low[at, cols], preferred_element_type=jnp.float32)
            into = total(g, m)
            if begun[g, n] > 1:
                into[...] += add
            else:
                into[...] = add
            if begun[g, n] == SIDE:
                write(g, m).start()

    seen = set()
    first_left = sum(n[0] in WEIGHTS and n[1] < 2 for n in copies)

    def follow(name):
        seen.add(name)
        for other, (_, after, _) in copies.items():
            if other not in started and name in after and all(n in seen for n in after):
                start(other)

    for act, name in schedule(copies):
        if act == "unit":
            multiply(*name)
            continue
        if act == "slot":
            slot_group(name)
            follow((act, name))
            continue
        copy(name).wait_recv()
        kind = name[0]
        if kind == "mirror":
            cols = pl.ds(columns(name[1]), wide(name[1]))
            mine = chunk(name[1], 0, 0, 0)
            weights[mine] = stored[:, cols] + parity * mirrored[name[1]]
        follow(name)
        if kind == "mirror":
            split(mine, CHUNK)
        if kind in WEIGHTS:
            h, s = name[1], name[-1]
            if kind == "line":
                split(chunk(h, -s, 0, 0), CHUNK)
            elif kind == "linepass":
                split(chunk(h, -2 * s, 0, s), CHUNK // 2)
            elif kind == "plane":
                split(chunk(h, name[2], -s, 0), CHUNK)
            else:
                split(chunk(h, name[2], -2 * s, s), CHUNK // 2)
            if h < 2:
                first_left -= 1
                if first_left == 0:
                    for n in copies:
                        if n[0] in WEIGHTS and n[1] < 2:
                            copy(n).wait_send()

    for n in copies:
        if n[0] == "meta":
            copy(n).wait_recv()
    for i in range(16):
        meta[i] = heard[i]
    for n in copies:
        if n[0] not in WEIGHTS or n[1] >= 2:
            copy(n).wait_send()
    for g in range(SIDE):
        for m in range(TILES):
            write(g, m).wait()


def exchange(amp, own, gap, irrep, stored, flags):
    n = len(plan())
    vmem = pl.BlockSpec(memory_space=pltpu.VMEM)
    return pl.pallas_call(
        kernel,
        out_shape=(
            jax.ShapeDtypeStruct((16 * CAP, LANES), jnp.float32),
            jax.ShapeDtypeStruct((16, 8, CAP), jnp.float32),
        ),
        in_specs=[pl.BlockSpec(memory_space=pl.ANY)] + [vmem] * 4 + [pl.BlockSpec(memory_space=pltpu.SMEM)],
        out_specs=(pl.BlockSpec(memory_space=pl.ANY), vmem),
        scratch_shapes=[
            pltpu.VMEM((SIDE * CORES, 16, CAP, PART), jnp.float32),
            pltpu.VMEM((PIECES, DEPTH, TILE), jnp.float32),
            pltpu.VMEM((DEPTH, LANES), jnp.bfloat16),
            pltpu.VMEM((DEPTH, LANES), jnp.bfloat16),
            pltpu.VMEM((ROWS, PART), jnp.bfloat16),
            pltpu.VMEM((ROWS, PART), jnp.bfloat16),
            pltpu.VMEM((TILES, GROUP, TILE), jnp.float32),
            pltpu.VMEM((16, CAP, PART), jnp.float32),
            pltpu.VMEM((PIECES, CHUNK, TILE), jnp.float32),
            pltpu.VMEM((16, ROWS), jnp.float32),
            pltpu.VMEM((16, 8, CAP), jnp.float32),
            pltpu.VMEM((16, 8, CAP), jnp.float32),
            pltpu.SemaphoreType.DMA((n,)),
            pltpu.SemaphoreType.DMA((n,)),
            pltpu.SemaphoreType.DMA((SIDE * TILES + 1,)),
        ],
        compiler_params=pltpu.CompilerParams(
            collective_id=0, has_side_effects=True, vmem_limit_bytes=60 * 2**20
        ),
        name="exchange",
    )(amp, own, gap, irrep, stored, flags)


def per_device(amplitudes, row_gap, row_irrep, owners, stored, col_gap, col_irrep, mirror_flags):
    line = (1, ROWS)
    cycle, meta = exchange(
        amplitudes.reshape(ROWS // CAP, CAP, PART), owners.reshape(line), row_gap.reshape(line), row_irrep.reshape(line), stored, mirror_flags
    )
    gap = (meta[:, 0] + meta[:, 1] + meta[:, 2]).reshape(-1, 1)
    irrep = (meta[:, 3] - 1.0).reshape(-1, 1)
    same = irrep == col_irrep.astype(jnp.float32)[None, :]
    return jnp.where(same, cycle / (gap + col_gap[None, :]), 0.0)


def solution(mesh):
    placed = (
        P("row", "col"),
        P("row"),
        P("row"),
        P("row", None),
        P("row", "col"),
        P("col"),
        P("col"),
        P(),
    )
    return jax.shard_map(
        per_device, mesh=mesh, in_specs=placed, out_specs=P("row", "col"), check_vma=False
    )
```
